32 devices in a mesh: kz: 4 (over x, core), en: 8 (over z, y).
Axes of the slice: x: 2, y: 2, z: 4, core: 2. Of those that a mesh axis runs over, the one named last changes fastest.
Arguments:
- green_blocks: float32 [4, 16, 2, 256, 256], P('kz', 'en'), may hold values from -6 to 6
- couplings: float32 [4, 8, 2, 256, 256], P('kz', 'en'), may hold values from -0.375 to 0.375
- owners: int32 [2], replicated, may hold values from 0 to 31
- momentum_shift: int32 [2], replicated, may hold values from -3 to 3
- energy_shift: int32 [2], replicated, may hold values from 1 to 7
Outputs:
- self_energy: float32 [4, 16, 2, 256, 256], P('kz', 'en')
The draws below stay inside these ranges and needn't reach their ends.
Inputs may be any that keep to these rules, and one draw needn't show every extreme that they name: `owners`: flat device index of each mode's coupling block.
All inputs are finite; a program needn't handle non-finite values.
Results may differ from the reference program's by a relative error of at most 0.0001.
Values sent between devices are 32-bit elements; how exact they have to be, the bound alone decides.
No kernel may reach another device: no remote copies, remote signals or barrier semaphores. Data moves between devices by JAX's collectives and lax.ppermute only.
A program may use at most 64 MiB of HBM per device.

```python
import jax
import jax.numpy as jnp
from jax import lax

NB = 256
ED = 2
MODES = 2
NK = 4
NE = 16
N_KZ = 4
N_EN = 8


def block_scale(rng, shape, split, low, top_value):
    def one(position, blocks):
        draws = jax.random.uniform(jax.random.fold_in(jax.random.fold_in(rng, 6), position), (blocks,), jnp.float32, low / len(split), top_value / len(split))
        return jnp.repeat(jnp.exp(draws), shape[position] // blocks).reshape((-1,) + (1,) * (len(shape) - position - 1))

    gain = one(*split[0])
    for cut in split[1:]:
        gain = gain * one(*cut)
    return gain


def scatter_about(own_key, extent, scale, bound, pieces=(), kind=jnp.bfloat16):
    entries = scale * jax.random.normal(own_key, extent, jnp.float32)
    if pieces:
        entries = entries * block_scale(own_key, extent, pieces, -0.22, 0.18)
    return jnp.clip(entries, -bound, bound).astype(kind)


def setup_inputs(seed: int = 0) -> dict:
    arg_keys = jax.random.split(jax.random.key(seed), 6)
    green_blocks = scatter_about(arg_keys[0], (NK, NE, 2, NB, NB), 1.0, 6.0, ((0, 4), (1, 8)), jnp.float32)
    couplings = scatter_about(arg_keys[1], (N_KZ, N_EN, 2, NB, NB), NB ** -0.5, 0.375, ((0, 4), (1, 8)), jnp.float32)
    owners = jax.random.randint(arg_keys[2], (MODES,), 0, N_KZ * N_EN).astype(jnp.int32)
    momentum_shift = jax.random.randint(arg_keys[3], (MODES,), 1 - NK, NK).astype(jnp.int32)
    energy_shift = jax.random.randint(arg_keys[4], (MODES,), 1, 4 * ED).astype(jnp.int32)
    return dict(green_blocks=green_blocks, couplings=couplings, owners=owners, momentum_shift=momentum_shift, energy_shift=energy_shift)


def matmul_left(left, right):
    return jnp.einsum("ij,...jk->...ik", left, right, precision=lax.Precision.HIGHEST)


def matmul_right(left, right):
    return jnp.einsum("...ij,kj->...ik", left, right, precision=lax.Precision.HIGHEST)


def sandwich(coupling, blocks):
    couple_real = coupling[0]
    couple_imag = coupling[1]
    green_real = blocks[..., 0, :, :]
    green_imag = blocks[..., 1, :, :]
    left_real = matmul_left(couple_real, green_real) - matmul_left(couple_imag, green_imag)
    left_imag = matmul_left(couple_real, green_imag) + matmul_left(couple_imag, green_real)
    out_real = matmul_right(left_real, couple_real) + matmul_right(left_imag, couple_imag)
    out_imag = matmul_right(left_imag, couple_real) - matmul_right(left_real, couple_imag)
    return jnp.stack([out_real, out_imag], axis=-3)


def reference(green_blocks, couplings, owners, momentum_shift, energy_shift):
    flat_table = couplings.reshape(N_KZ * N_EN, 2, NB, NB)
    result = jnp.zeros(green_blocks.shape, jnp.float32)
    for mode_index in range(MODES):
        coupling = lax.dynamic_index_in_dim(flat_table, owners[mode_index].astype(jnp.int32), 0, keepdims=False)
        rolled = jnp.roll(green_blocks, momentum_shift[mode_index], axis=0)
        padded = jnp.pad(rolled, ((0, 0), (NE, 0), (0, 0), (0, 0), (0, 0)))
        start = (NE - energy_shift[mode_index]).astype(jnp.int32)
        shifted = lax.dynamic_slice_in_dim(padded, start, NE, 1)

        def one_momentum(blocks):
            return sandwich(coupling, blocks)

        result = result + lax.map(one_momentum, shifted)
    return result
```

```python
import jax
import jax.numpy as jnp
from jax import lax
from jax.experimental import pallas as pl
from jax.experimental.pallas import tpu as pltpu
from jax.sharding import PartitionSpec as P

AXES = ("kz", "en")
MAX_SHIFT = 7
MAX_BRANCHES = 64


def sizes():
    return lax.axis_size("kz"), lax.axis_size("en")


def pairs_shift(momentum, energy):
    n_kz, n_en = sizes()
    return [
        (k * n_en + d, (k + momentum) % n_kz * n_en + d + energy)
        for k in range(n_kz)
        for d in range(n_en)
        if d + energy < n_en
    ]


def pairs_flip(kz_bits, en_bits):
    n_kz, n_en = sizes()
    return [(k * n_en + d, (k ^ kz_bits) * n_en + (d ^ en_bits)) for k in range(n_kz) for d in range(n_en)]


def flip(array, kz_bits, en_bits):
    return lax.ppermute(array, AXES, pairs_flip(kz_bits, en_bits))


def shift_blocks(blocks, momentum, energy):
    count = len(blocks)
    out = []
    for place in range(count):
        source = (place - energy) % count
        steps = (energy - place + source) // count
        if momentum == 0 and steps == 0:
            out.append(blocks[source])
        else:
            out.append(lax.ppermute(blocks[source], AXES, pairs_shift(momentum, steps)))
    return tuple(out)


def move(blocks, momentum, energy, low, high, extra, operands):
    n_kz, _ = sizes()
    count = high - low + 1

    def branch(q, e):
        return lambda held, ops: (shift_blocks(held, q, e), extra(*ops))

    if n_kz * count <= MAX_BRANCHES:
        branches = [branch(q, e) for q in range(n_kz) for e in range(low, high + 1)]
        return lax.switch(momentum * count + energy - low, branches, blocks, operands)
    blocks, more = lax.switch(energy - low, [branch(0, e) for e in range(low, high + 1)], blocks, operands)
    for bit in range((n_kz - 1).bit_length()):
        blocks = lax.cond(
            (momentum >> bit) % 2 == 1,
            lambda held, bit=bit: shift_blocks(held, 1 << bit, 0),
            lambda held: held,
            blocks,
        )
    return blocks, more


def position():
    k, d = lax.axis_index("kz"), lax.axis_index("en")
    return k % 2, k // 2 % 2 * 2 + d % 2


def scatter_couplings(own, owner_kz, owner_en):
    n_kz, n_en = sizes()
    core, chip = position()
    k, d = lax.axis_index("kz"), lax.axis_index("en")
    parts, rows, columns = own.shape
    quarter = rows // 4
    theirs = flip(lax.dynamic_index_in_dim(own, 1 - core, 0, keepdims=False), 1, 0)
    mine = lax.dynamic_index_in_dim(own, core, 0, keepdims=False)

    def piece(which):
        here = lax.dynamic_slice_in_dim(mine, which * quarter, quarter, 0)
        there = lax.dynamic_slice_in_dim(theirs, which * quarter, quarter, 0)
        return jnp.where((owner_kz % 2 == core)[:, None, None], here[None], there[None])

    far = {j: flip(piece(chip ^ j), j // 2 * 2, j % 2) for j in (3, 2, 1)}
    holder = ((owner_kz // 2 % 2 * 2 + owner_en % 2) ^ chip)[:, None, None]
    value = piece(chip)
    for j in (1, 2, 3):
        value = jnp.where(holder == j, far[j], value)
    return value


def spread_rest(value, owner_kz, owner_en, kz_bits, en_bits):
    k, d = lax.axis_index("kz"), lax.axis_index("en")
    for bit in en_bits:
        other = flip(value, 0, 1 << bit)
        value = jnp.where(((owner_en >> bit) % 2 == (d >> bit) % 2)[:, None, None], value, other)
    for bit in kz_bits:
        other = flip(value, 1 << bit, 0)
        value = jnp.where(((owner_kz >> bit) % 2 == (k >> bit) % 2)[:, None, None], value, other)
    return value


def gather_couplings(value):
    held = [value] + [None] * 3
    for j in (3, 2, 1):
        held[j] = flip(value, j // 2 * 2, j % 2)
    return tuple(held) + tuple(flip(piece, 1, 0) for piece in held)


def dot(left, right):
    return jnp.dot(left, right, preferred_element_type=jnp.float32)


def dot_nt(left, right):
    return lax.dot_general(left, right, (((1,), (1,)), ((), ())), preferred_element_type=jnp.float32)


def split(value):
    high = value.astype(jnp.bfloat16)
    return high, (value - high.astype(jnp.float32)).astype(jnp.bfloat16)


def kernel(place, *refs):
    pieces, blocks, out, high, low = refs[:8], refs[8:12], refs[12], refs[13], refs[14]
    core, chip = place[0], place[1]
    size = out.shape[-1]
    for half in range(2):
        for j in range(4):
            for mode in range(2):
                top, rest = split(pieces[half * 4 + j][mode])
                high[mode, core ^ half, chip ^ j] = top
                low[mode, core ^ half, chip ^ j] = rest
    for local in range(2):
        total_real = total_imag = None
        for mode in range(2):
            vrh, vih = (high[mode, part].reshape(size, size) for part in range(2))
            vrl, vil = (low[mode, part].reshape(size, size) for part in range(2))
            block = blocks[mode * 2 + local]
            grh, grl = split(block[0, 0, 0])
            gih, gil = split(block[0, 0, 1])
            left = jnp.concatenate([vrh, vrh, vrl, vih, vih, vil], axis=1)
            real = dot(left, jnp.concatenate([grh, grl, grh, -gih, -gil, -gih], axis=0))
            imag = dot(left, jnp.concatenate([gih, gil, gih, grh, grl, grh], axis=0))
            rh, rl = split(real)
            ih, il = split(imag)
            right = jnp.concatenate([vrh, vrl, vrh, vih, vil, vih], axis=1)
            out_real = dot_nt(jnp.concatenate([rh, rh, rl, ih, ih, il], axis=1), right)
            out_imag = dot_nt(jnp.concatenate([ih, ih, il, -rh, -rh, -rl], axis=1), right)
            total_real = out_real if total_real is None else total_real + out_real
            total_imag = out_imag if total_imag is None else total_imag + out_imag
        out[0, local, 0] = total_real
        out[0, local, 1] = total_imag


def sandwich_sum(place, pieces, blocks, shape):
    size = shape[-1]
    vmem = pl.BlockSpec(memory_space=pltpu.VMEM)
    return pl.pallas_call(
        kernel,
        out_shape=jax.ShapeDtypeStruct(shape, jnp.float32),
        in_specs=[pl.BlockSpec(memory_space=pltpu.SMEM)] + [vmem] * 12,
        out_specs=vmem,
        scratch_shapes=[pltpu.VMEM((2, 2, 4, size // 4, size), jnp.bfloat16)] * 2,
        cost_estimate=pl.CostEstimate(flops=192 * size**3, bytes_accessed=16 * size * size * 4, transcendentals=0),
        name="sandwich_sum",
    )(place, *pieces, *blocks)


def shards(green_blocks, couplings, owners, momentum_shift, energy_shift):
    n_kz, n_en = sizes()
    local = green_blocks.shape[1]
    swap = energy_shift[0] > energy_shift[1]
    first, second = jnp.where(swap, 1, 0), jnp.where(swap, 0, 1)
    order = jnp.stack([first, second])
    owner = owners[order]
    owner_kz, owner_en = owner // n_en, owner % n_en
    q_first = jnp.mod(momentum_shift[first], n_kz)
    q_more = jnp.mod(momentum_shift[second] - momentum_shift[first], n_kz)
    e_first = energy_shift[first]
    e_more = energy_shift[second] - e_first
    own = couplings[0, 0]
    blocks = tuple(green_blocks[:, i : i + 1] for i in range(local))
    en_rest = list(range(1, (n_en - 1).bit_length()))
    kz_rest = list(range(2, (n_kz - 1).bit_length()))

    def early(own, owner_kz, owner_en):
        value = scatter_couplings(own, owner_kz, owner_en)
        return spread_rest(value, owner_kz, owner_en, [], en_rest[:1])

    def late(value, owner_kz, owner_en):
        value = spread_rest(value, owner_kz, owner_en, kz_rest, en_rest[1:])
        return gather_couplings(value)

    near, value = move(blocks, q_first, e_first, 1, MAX_SHIFT, early, (own, owner_kz, owner_en))
    far, pieces = move(near, q_more, e_more, 0, MAX_SHIFT - 1, late, (value, owner_kz, owner_en))
    place = jnp.stack(position()).astype(jnp.int32)
    return sandwich_sum(place, pieces, near + far, green_blocks.shape)


def solution(mesh):
    in_specs = (P("kz", "en", None, None, None), P("kz", "en", None, None, None), P(), P(), P())
    out_specs = P("kz", "en", None, None, None)
    return jax.shard_map(shards, mesh=mesh, in_specs=in_specs, out_specs=out_specs, check_vma=False)
```

```python
import jax
import jax.numpy as jnp
from jax import lax
from jax.experimental import pallas as pl
from jax.experimental.pallas import tpu as pltpu
from jax.sharding import PartitionSpec as P


AXES = ("kz", "en")
MAX_SHIFT = 7
MAX_BRANCHES = 64


def sizes():
    return lax.axis_size("kz"), lax.axis_size("en")


def pairs_shift(momentum, energy):
    n_kz, n_en = sizes()
    return [
        (k * n_en + d, (k + momentum) % n_kz * n_en + d + energy)
        for k in range(n_kz)
        for d in range(n_en)
        if d + energy < n_en
    ]


def pairs_flip(kz_bits, en_bits):
    n_kz, n_en = sizes()
    return [(k * n_en + d, (k ^ kz_bits) * n_en + (d ^ en_bits)) for k in range(n_kz) for d in range(n_en)]


def flip(array, kz_bits, en_bits):
    return lax.ppermute(array, AXES, pairs_flip(kz_bits, en_bits))


def shift_blocks(blocks, momentum, energy):
    count = len(blocks)
    out = []
    for place in reversed(range(count)):
        source = (place - energy) % count
        steps = (energy - place + source) // count
        if momentum == 0 and steps == 0:
            out.append(blocks[source])
        else:
            out.append(lax.ppermute(blocks[source], AXES, pairs_shift(momentum, steps)))
    return tuple(reversed(out))


def move(blocks, momentum, energy, low, high, ride, operands):
    n_kz, _ = sizes()
    count = high - low + 1

    def branch(q, e):
        def run(held, ops):
            held, ops = ride(held, ops)
            return shift_blocks(held, q, e), ops

        return run

    if n_kz * count <= MAX_BRANCHES:
        branches = [branch(q, e) for q in range(n_kz) for e in range(low, high + 1)]
        return lax.switch(momentum * count + energy - low, branches, blocks, operands)
    blocks, more = lax.switch(energy - low, [branch(0, e) for e in range(low, high + 1)], blocks, operands)
    for bit in range((n_kz - 1).bit_length()):
        blocks = lax.cond(
            bit_of(momentum, bit) == 1,
            lambda held, bit=bit: shift_blocks(held, 1 << bit, 0),
            lambda held: held,
            blocks,
        )
    return blocks, more


def bit_of(number, bit):
    return lax.bitwise_and(lax.shift_right_logical(number, jnp.int32(bit)), jnp.int32(1))


def position():
    k, d = lax.axis_index("kz"), lax.axis_index("en")
    return bit_of(k, 0), 2 * bit_of(k, 1) + bit_of(d, 0)


def scatter_couplings(own, owners):
    core, chip = position()
    _, rows, _ = own.shape
    quarter = rows // 4
    n_en_bits = (sizes()[1] - 1).bit_length()
    theirs = flip(lax.dynamic_index_in_dim(own, 1 - core, 0, keepdims=False), 1, 0)
    mine = lax.dynamic_index_in_dim(own, core, 0, keepdims=False)

    def piece(which):
        here = lax.dynamic_slice_in_dim(mine, which * quarter, quarter, 0)
        there = lax.dynamic_slice_in_dim(theirs, which * quarter, quarter, 0)
        return jnp.stack([jnp.where(bit_of(owner, n_en_bits) == core, here, there) for owner in owners])

    far = {j: flip(piece(chip ^ j), j // 2 * 2, j % 2) for j in (3, 2, 1)}
    value = piece(chip)
    out = []
    for mode, owner in enumerate(owners):
        holder = (2 * bit_of(owner, n_en_bits + 1) + bit_of(owner, 0)) ^ chip
        chosen = value[mode]
        for j in (1, 2, 3):
            chosen = jnp.where(holder == j, far[j][mode], chosen)
        out.append(chosen)
    return jnp.stack(out)


def spread_bit(value, owners, axis, bit):
    here = bit_of(lax.axis_index(axis), bit)
    shift = 0 if axis == "en" else (sizes()[1] - 1).bit_length()
    other = flip(value, 0, 1 << bit) if axis == "en" else flip(value, 1 << bit, 0)
    return jnp.stack(
        [jnp.where(bit_of(owner, shift + bit) == here, value[mode], other[mode]) for mode, owner in enumerate(owners)]
    )


def dot(left, right):
    return jnp.dot(left, right, preferred_element_type=jnp.float32)


def dot_nt(left, right):
    return lax.dot_general(left, right, (((1,), (1,)), ((), ())), preferred_element_type=jnp.float32)


def split(value):
    high = value.astype(jnp.bfloat16)
    return high, (value - high.astype(jnp.float32)).astype(jnp.bfloat16)


def kernel(place, *refs):
    near, blocks, out = refs[:5], refs[5:9], refs[9]
    high, low, green_high, green_low = refs[10:]
    pieces = (near[:4], [near[4].at[j] for j in range(4)])
    core, chip = place[0], place[1]
    size = out.shape[-1]
    for mode in range(2):
        for half in range(2):
            for j in range(4):
                top, rest = split(pieces[half][j][place[2] ^ mode])
                high[mode, core ^ half, chip ^ j] = top
                low[mode, core ^ half, chip ^ j] = rest
    for mode in range(2):
        for local in range(2):
            for part in range(2):
                top, rest = split(blocks[mode * 2 + local][0, 0, part])
                green_high[mode * 2 + local, part] = top
                green_low[mode * 2 + local, part] = rest
    out[...] = jnp.zeros_like(out)

    def step(index, _):
        mode, local = index // 2, index % 2
        vrh, vih = (high[mode, part].reshape(size, size) for part in range(2))
        vrl, vil = (low[mode, part].reshape(size, size) for part in range(2))
        grh, gih = green_high[index, 0], green_high[index, 1]
        grl, gil = green_low[index, 0], green_low[index, 1]
        left = jnp.concatenate([vrh, vrh, vrl, vih, vih, vil], axis=1)
        real = dot(left, jnp.concatenate([grh, grl, grh, -gih, -gil, -gih], axis=0))
        imag = dot(left, jnp.concatenate([gih, gil, gih, grh, grl, grh], axis=0))
        rh, rl = split(real)
        ih, il = split(imag)
        right = jnp.concatenate([vrh, vrl, vrh, vih, vil, vih], axis=1)
        out[0, local, 0] += dot_nt(jnp.concatenate([rh, rh, rl, ih, ih, il], axis=1), right)
        out[0, local, 1] += dot_nt(jnp.concatenate([ih, ih, il, -rh, -rh, -rl], axis=1), right)
        return 0

    lax.fori_loop(0, 4, step, 0)


def sandwich_sum(place, pieces, blocks, shape):
    size = shape[-1]
    vmem = pl.BlockSpec(memory_space=pltpu.VMEM)
    return pl.pallas_call(
        kernel,
        out_shape=jax.ShapeDtypeStruct(shape, jnp.float32),
        in_specs=[pl.BlockSpec(memory_space=pltpu.SMEM)] + [vmem] * 9,
        out_specs=vmem,
        scratch_shapes=[pltpu.VMEM((2, 2, 4, size // 4, size), jnp.bfloat16)] * 2
        + [pltpu.VMEM((4, 2, size, size), jnp.bfloat16)] * 2,
        cost_estimate=pl.CostEstimate(flops=192 * size**3, bytes_accessed=16 * size * size * 4, transcendentals=0),
        name="sandwich_sum",
    )(place, *pieces, *blocks)


def shards(green_blocks, couplings, owners, momentum_shift, energy_shift):
    n_kz, n_en = sizes()
    local = green_blocks.shape[1]
    assert n_kz & (n_kz - 1) == 0 and n_en & (n_en - 1) == 0
    swap = energy_shift[0] > energy_shift[1]
    e_first, e_second = jnp.minimum(energy_shift[0], energy_shift[1]), jnp.maximum(energy_shift[0], energy_shift[1])
    q_first = jnp.where(swap, momentum_shift[1], momentum_shift[0])
    q_more = jnp.where(swap, momentum_shift[0], momentum_shift[1]) - q_first
    q_first, q_more = q_first & (n_kz - 1), q_more & (n_kz - 1)
    e_more = e_second - e_first
    owner = (owners[0], owners[1])
    blocks = tuple(green_blocks[:, i : i + 1] for i in range(local))
    en_rest = [("en", bit) for bit in range(1, (n_en - 1).bit_length())]
    rest = en_rest + [("kz", bit) for bit in range(2, (n_kz - 1).bit_length())]

    value = scatter_couplings(couplings[0, 0], owner)

    def early(held, ops):
        value, owner = ops
        for step, (axis, bit) in enumerate(rest):
            value = spread_bit(value, owner, axis, bit)
            if step == 0:
                last, value = lax.optimization_barrier((held[-1], value))
                held = held[:-1] + (last,)
        return held, value

    def late(held, value):
        pieces = [value] + [None] * 3
        for j in (3, 2, 1):
            pieces[j] = flip(value, j // 2 * 2, j % 2)
        return held, tuple(pieces) + (flip(jnp.stack(pieces), 1, 0),)

    blocks, q_more, e_more, q_first, e_first = lax.optimization_barrier((blocks, q_more, e_more, q_first, e_first))
    near, value = move(blocks, q_first, e_first, 1, MAX_SHIFT, early, (value, owner))
    far, pieces = move(near, q_more, e_more, 0, MAX_SHIFT - 1, late, value)
    place = jnp.stack([*position(), swap.astype(jnp.int32)])
    return sandwich_sum(place, pieces, near + far, green_blocks.shape)


def solution(mesh):
    in_specs = (P("kz", "en", None, None, None), P("kz", "en", None, None, None), P(), P(), P())
    out_specs = P("kz", "en", None, None, None)
    return jax.shard_map(shards, mesh=mesh, in_specs=in_specs, out_specs=out_specs, check_vma=False)
```

```python
import jax
import jax.numpy as jnp
from jax import lax
from jax.experimental import pallas as pl
from jax.experimental.pallas import tpu as pltpu
from jax.sharding import PartitionSpec as P


AXES = ("kz", "en")
MAX_SHIFT = 7
MAX_BRANCHES = 64


def sizes():
    return lax.axis_size("kz"), lax.axis_size("en")


def pairs_shift(momentum, energy):
    n_kz, n_en = sizes()
    return [
        (k * n_en + d, (k + momentum) % n_kz * n_en + d + energy)
        for k in range(n_kz)
        for d in range(n_en)
        if d + energy < n_en
    ]


def pairs_flip(kz_bits, en_bits):
    n_kz, n_en = sizes()
    return [(k * n_en + d, (k ^ kz_bits) * n_en + (d ^ en_bits)) for k in range(n_kz) for d in range(n_en)]


def flip(array, kz_bits, en_bits):
    return lax.ppermute(array, AXES, pairs_flip(kz_bits, en_bits))


def shift_blocks(blocks, momentum, energy):
    count = len(blocks)
    out = []
    for place in reversed(range(count)):
        source = (place - energy) % count
        steps = (energy - place + source) // count
        if momentum == 0 and steps == 0:
            out.append(blocks[source])
        else:
            out.append(lax.ppermute(blocks[source], AXES, pairs_shift(momentum, steps)))
    return tuple(reversed(out))


def move(blocks, index, low, ride, operands):
    n_kz, _ = sizes()

    def branch(q, e):
        def run(held, ops):
            held, ops = ride(held, ops)
            return shift_blocks(held, q, e + low), ops

        return run

    if n_kz * MAX_SHIFT <= MAX_BRANCHES:
        branches = [branch(q, e) for q in range(n_kz) for e in range(MAX_SHIFT)]
        return lax.switch(index, branches, blocks, operands)
    momentum = index // MAX_SHIFT
    blocks, more = lax.switch(index - momentum * MAX_SHIFT, [branch(0, e) for e in range(MAX_SHIFT)], blocks, operands)
    for bit in range((n_kz - 1).bit_length()):
        blocks = lax.cond(
            bit_of(momentum, bit) == 1,
            lambda held, bit=bit: shift_blocks(held, 1 << bit, 0),
            lambda held: held,
            blocks,
        )
    return blocks, more


def bit_of(number, bit):
    return (number >> bit) & 1


def bits_of(numbers, bit, value):
    return (bit_of(numbers, bit) == value)[:, None, None]


def position():
    k, d = lax.axis_index("kz"), lax.axis_index("en")
    return bit_of(k, 0), 2 * bit_of(k, 1) + bit_of(d, 0)


def part_of_both_cores(own):
    core, _ = position()
    theirs = flip(lax.dynamic_index_in_dim(own, 1 - core, 0, keepdims=False), 1, 0)
    return lax.dynamic_index_in_dim(own, core, 0, keepdims=False), theirs


def cut_couplings(mine, theirs, owners):
    core, chip = position()
    quarter = mine.shape[0] // 4
    from_core = bits_of(owners, (sizes()[1] - 1).bit_length(), core)

    def piece(which):
        here = lax.dynamic_slice_in_dim(mine, which * quarter, quarter, 0)
        there = lax.dynamic_slice_in_dim(theirs, which * quarter, quarter, 0)
        return jnp.where(from_core, here[None], there[None])

    return tuple(piece(chip ^ j) for j in range(4))


def scatter_couplings(pieces, owners):
    _, chip = position()
    far = {j: flip(pieces[j], j // 2 * 2, j % 2) for j in (3, 2, 1)}
    holder = ((2 * bit_of(owners, (sizes()[1] - 1).bit_length() + 1) + bit_of(owners, 0)) ^ chip)[:, None, None]
    value = pieces[0]
    for j in (1, 2, 3):
        value = jnp.where(holder == j, far[j], value)
    return value


def send_bit(value, axis, bit):
    return flip(value, 0, 1 << bit) if axis == "en" else flip(value, 1 << bit, 0)


def keep_bit(value, other, owners, axis, bit):
    shift = 0 if axis == "en" else (sizes()[1] - 1).bit_length()
    return jnp.where(bits_of(owners, shift + bit, bit_of(lax.axis_index(axis), bit)), value, other)


def dot(left, right):
    return jnp.dot(left, right, preferred_element_type=jnp.float32)


def dot_nt(left, right):
    return lax.dot_general(left, right, (((1,), (1,)), ((), ())), preferred_element_type=jnp.float32)


def split(value):
    high = value.astype(jnp.bfloat16)
    return high, (value - high.astype(jnp.float32)).astype(jnp.bfloat16)


def kernel(energy, *refs):
    near, blocks, out = refs[:5], refs[5:9], refs[9]
    coupling, green, sums, cut, sems, block_sems, out_sems = refs[10:]
    core, chip = position()
    swap = (energy[0] > energy[1]).astype(jnp.int32)
    quarter, size = coupling.shape[-2:]
    loads = [pltpu.make_async_copy(near[j], coupling.at[0, j], sems.at[j]) for j in range(4)]
    loads.append(pltpu.make_async_copy(near[4], coupling.at[1], sems.at[4]))
    for load in loads:
        load.start()
    for local in range(2):
        for mode in range(2):
            place = local * 2 + mode
            pltpu.make_async_copy(blocks[mode * 2 + local].at[0, 0], green.at[place], block_sems.at[place]).start()
    sums[...] = jnp.zeros_like(sums)
    for load in loads:
        load.wait()
    for mode in range(2):
        for j in range(4):
            rows = pl.ds(pl.multiple_of((chip ^ j) * quarter, quarter), quarter)
            real = coupling[core, j, swap ^ mode]
            imag = coupling[1 - core, j, swap ^ mode]
            for which, value in enumerate((real, imag, real + imag)):
                top, rest = split(value)
                cut[mode, which, rows, 0:size] = top
                cut[mode, which, rows, size : 2 * size] = top
                cut[mode, which, rows, 2 * size : 3 * size] = rest

    def left(mode, which, value):
        top, rest = split(value)
        return dot(cut[mode, which], jnp.concatenate([top, rest, top], axis=0))

    def right(mode, which, value):
        top, rest = split(value)
        return dot_nt(jnp.concatenate([top, rest, top], axis=1), cut[mode, which])

    def step(place, _):
        local, mode = place // 2, place % 2
        pltpu.make_async_copy(blocks[0].at[0, 0], green.at[place], block_sems.at[place]).wait()
        real, imag = green[place, 0], green[place, 1]
        first = left(mode, 0, real)
        second = left(mode, 1, imag)
        both = left(mode, 2, real + imag)
        real, imag = first - second, both - first - second
        first = right(mode, 0, real)
        second = right(mode, 1, imag)
        sums[local, 0] += first + second
        sums[local, 1] += first - second
        sums[local, 1] += right(mode, 2, imag - real)

        @pl.when(mode == 1)
        def _():
            pltpu.make_async_copy(sums.at[local], out.at[0, local], out_sems.at[local]).start()

        return 0

    lax.fori_loop(0, 4, step, 0)
    for local in range(2):
        pltpu.make_async_copy(sums.at[local], out.at[0, local], out_sems.at[local]).wait()


def sandwich_sum(energy, pieces, blocks, shape):
    size = shape[-1]
    anywhere = pl.BlockSpec(memory_space=pl.ANY)
    return pl.pallas_call(
        kernel,
        out_shape=jax.ShapeDtypeStruct(shape, jnp.float32),
        in_specs=[pl.BlockSpec(memory_space=pltpu.SMEM)] + [anywhere] * 9,
        out_specs=anywhere,
        scratch_shapes=[
            pltpu.VMEM((2, 4, 2, size // 4, size), jnp.float32),
            pltpu.VMEM((4, 2, size, size), jnp.float32),
            pltpu.VMEM((2, 2, size, size), jnp.float32),
            pltpu.VMEM((2, 3, size, 3 * size), jnp.bfloat16),
            pltpu.SemaphoreType.DMA((5,)),
            pltpu.SemaphoreType.DMA((4,)),
            pltpu.SemaphoreType.DMA((2,)),
        ],
        cost_estimate=pl.CostEstimate(flops=144 * size**3, bytes_accessed=16 * size * size * 4, transcendentals=0),
        name="sandwich_sum",
    )(energy, *pieces, *blocks)


def shards(green_blocks, couplings, owners, momentum_shift, energy_shift):
    n_kz, n_en = sizes()
    local = green_blocks.shape[1]
    pieces = cut_couplings(*part_of_both_cores(couplings[0, 0]), owners)
    pieces, green_blocks = lax.optimization_barrier((pieces, green_blocks))
    value = scatter_couplings(pieces, owners)
    assert n_kz & (n_kz - 1) == 0 and n_en & (n_en - 1) == 0
    count = MAX_SHIFT
    energy, momentum = energy_shift, momentum_shift
    energy_other, momentum_other = energy[::-1], momentum[::-1]
    low, high = jnp.minimum(energy, energy_other), jnp.maximum(energy, energy_other)
    first = jnp.where(energy > energy_other, momentum_other, momentum)
    more = jnp.where(energy_other > energy, momentum_other - momentum, momentum - momentum_other)
    lead = jnp.arange(2) == 0
    steps = jnp.where(lead, first, more) & (n_kz - 1)
    rise = jnp.where(lead, low - 1, high - low)
    index = steps * count + rise
    blocks = tuple(green_blocks[:, i : i + 1] for i in range(local))
    en_rest = [("en", bit) for bit in range(1, (n_en - 1).bit_length())]
    rest = en_rest + [("kz", bit) for bit in range(2, (n_kz - 1).bit_length())]

    def early(held, ops):
        value, owner = ops
        for step, (axis, bit) in enumerate(rest):
            other = send_bit(value, axis, bit)
            value = keep_bit(value, other, owner, axis, bit)
            if step == 0:
                last, value = lax.optimization_barrier((held[-1], value))
                held = held[:-1] + (last,)
        return held, value

    def late(held, value):
        pieces = [value] + [None] * 3
        for j in (3, 2, 1):
            pieces[j] = flip(value, j // 2 * 2, j % 2)
        return held, tuple(pieces) + (flip(jnp.stack(pieces), 1, 0),)

    blocks, index_first, index_more = lax.optimization_barrier((blocks, index[0], index[1]))
    near, value = move(blocks, index_first, 1, early, (value, owners))
    far, pieces = move(near, index_more, 0, late, value)
    return sandwich_sum(energy_shift, pieces, near + far, green_blocks.shape)


def solution(mesh):
    in_specs = (P("kz", "en", None, None, None), P("kz", "en", None, None, None), P(), P(), P())
    out_specs = P("kz", "en", None, None, None)
    return jax.shard_map(shards, mesh=mesh, in_specs=in_specs, out_specs=out_specs, check_vma=False)
```

```python
import jax
import jax.numpy as jnp
from jax import lax
from jax.experimental import pallas as pl
from jax.experimental.pallas import tpu as pltpu
from jax.sharding import PartitionSpec as P


AXES = ("kz", "en")
MAX_SHIFT = 7
MAX_BRANCHES = 64


def sizes():
    return lax.axis_size("kz"), lax.axis_size("en")


def pairs_shift(momentum, energy):
    n_kz, n_en = sizes()
    return [
        (k * n_en + d, (k + momentum) % n_kz * n_en + (d + energy) % n_en) for k in range(n_kz) for d in range(n_en)
    ]


def pairs_flip(kz_bits, en_bits):
    n_kz, n_en = sizes()
    return [(k * n_en + d, (k ^ kz_bits) * n_en + (d ^ en_bits)) for k in range(n_kz) for d in range(n_en)]


def flip(array, kz_bits, en_bits):
    return lax.ppermute(array, AXES, pairs_flip(kz_bits, en_bits))


def shift_blocks(blocks, momentum, energy):
    count = len(blocks)
    out = []
    for place in reversed(range(count)):
        source = (place - energy) % count
        steps = (energy - place + source) // count
        if momentum == 0 and steps == 0:
            out.append(blocks[source])
        else:
            out.append(lax.ppermute(blocks[source], AXES, pairs_shift(momentum, steps)))
    return tuple(reversed(out))


def move(blocks, index, low, ride, operands):
    n_kz, _ = sizes()

    def branch(q, e):
        def run(held, ops):
            held, ops = ride(held, ops)
            return shift_blocks(held, q, e + low), ops

        return run

    if n_kz * MAX_SHIFT <= MAX_BRANCHES:
        branches = [branch(q, e) for q in range(n_kz) for e in range(MAX_SHIFT)]
        return lax.switch(index, branches, blocks, operands)
    momentum = index // MAX_SHIFT
    blocks, more = lax.switch(index - momentum * MAX_SHIFT, [branch(0, e) for e in range(MAX_SHIFT)], blocks, operands)
    for bit in range((n_kz - 1).bit_length()):
        blocks = lax.cond(
            bit_of(momentum, bit) == 1,
            lambda held, bit=bit: shift_blocks(held, 1 << bit, 0),
            lambda held: held,
            blocks,
        )
    return blocks, more


def bit_of(number, bit):
    return (number >> bit) & 1


def bits_of(numbers, bit, value):
    return (bit_of(numbers, bit) == value)[:, None, None]


def position():
    k, d = lax.axis_index("kz"), lax.axis_index("en")
    return bit_of(k, 0), 2 * bit_of(k, 1) + bit_of(d, 0)


def part_of_both_cores(own):
    core, _ = position()
    theirs = flip(lax.dynamic_index_in_dim(own, 1 - core, 0, keepdims=False), 1, 0)
    return lax.dynamic_index_in_dim(own, core, 0, keepdims=False), theirs


def cut_couplings(mine, theirs, owners):
    core, chip = position()
    quarter = mine.shape[0] // 4
    from_core = bits_of(owners, (sizes()[1] - 1).bit_length(), core)

    def piece(which):
        here = lax.dynamic_slice_in_dim(mine, which * quarter, quarter, 0)
        there = lax.dynamic_slice_in_dim(theirs, which * quarter, quarter, 0)
        return jnp.where(from_core, here[None], there[None])

    return tuple(piece(chip ^ j) for j in range(4))


def scatter_couplings(pieces, owners):
    _, chip = position()
    far = {j: flip(pieces[j], j // 2 * 2, j % 2) for j in (3, 2, 1)}
    holder = ((2 * bit_of(owners, (sizes()[1] - 1).bit_length() + 1) + bit_of(owners, 0)) ^ chip)[:, None, None]
    value = pieces[0]
    for j in (1, 2, 3):
        value = jnp.where(holder == j, far[j], value)
    return value


def send_bit(value, axis, bit):
    return flip(value, 0, 1 << bit) if axis == "en" else flip(value, 1 << bit, 0)


def keep_bit(value, other, owners, axis, bit):
    shift = 0 if axis == "en" else (sizes()[1] - 1).bit_length()
    return jnp.where(bits_of(owners, shift + bit, bit_of(lax.axis_index(axis), bit)), value, other)


def dot(left, right):
    return jnp.dot(left, right, preferred_element_type=jnp.float32)


def dot_nt(left, right):
    return lax.dot_general(left, right, (((1,), (1,)), ((), ())), preferred_element_type=jnp.float32)


def split(value):
    high = value.astype(jnp.bfloat16)
    return high, (value - high.astype(jnp.float32)).astype(jnp.bfloat16)


def kernel(energy, *refs):
    near, blocks, out = refs[:5], refs[5:9], refs[9]
    coupling, green, sums, cut, sems, block_sems, out_sems = refs[10:]
    core, chip = position()
    swap = (energy[0] > energy[1]).astype(jnp.int32)
    quarter, size = coupling.shape[-2:]
    loads = [pltpu.make_async_copy(near[j], coupling.at[0, j], sems.at[j]) for j in range(4)]
    loads.append(pltpu.make_async_copy(near[4], coupling.at[1], sems.at[4]))
    for load in loads:
        load.start()
    for place in range(4):
        pltpu.make_async_copy(blocks[place].at[0, 0], green.at[place], block_sems.at[place]).start()
    sums[...] = jnp.zeros_like(sums)
    for load in loads:
        load.wait()
    for mode in range(2):
        for j in range(4):
            rows = pl.ds(pl.multiple_of((chip ^ j) * quarter, quarter), quarter)
            real = coupling[core, j, swap ^ mode]
            imag = coupling[1 - core, j, swap ^ mode]
            for which, value in enumerate((real, imag, real + imag)):
                top, rest = split(value)
                cut[mode, which, rows, 0:size] = top
                cut[mode, which, rows, size : 2 * size] = top
                cut[mode, which, rows, 2 * size : 3 * size] = rest

    def left(mode, which, value):
        top, rest = split(value)
        return dot(cut[mode, which], jnp.concatenate([top, rest, top], axis=0))

    def right(mode, which, value):
        top, rest = split(value)
        return dot_nt(jnp.concatenate([top, rest, top], axis=1), cut[mode, which])

    lowest, highest = jnp.minimum(energy[0], energy[1]), jnp.maximum(energy[0], energy[1])
    base = lax.axis_index("en") * 2

    def step(mode, _):
        shift = jnp.where(mode == 0, lowest, highest)
        for local in range(2):
            place = mode * 2 + local
            pltpu.make_async_copy(blocks[0].at[0, 0], green.at[place], block_sems.at[place]).wait()
        pl.when(base + 1 >= shift)(lambda: add_term(mode, base >= shift))
        return 0

    def add_term(mode, lower):
        def pair(part):
            below = jnp.where(lower, green[mode * 2, part], 0.0)
            return jnp.concatenate([below, green[mode * 2 + 1, part]], axis=1)

        real, imag = pair(0), pair(1)
        first = left(mode, 0, real)
        second = left(mode, 1, imag)
        both = left(mode, 2, real + imag)
        real, imag = stacked(first - second), stacked(both - first - second)
        first = right(mode, 0, real)
        second = right(mode, 1, imag)
        add(0, first + second)
        add(1, first - second)
        add(1, right(mode, 2, imag - real))

    def stacked(value):
        return jnp.concatenate([value[:, :size], value[:, size:]], axis=0)

    def add(part, value):
        for local in range(2):
            sums[local, part] += value[local * size : (local + 1) * size]

    lax.fori_loop(0, 2, step, 0)
    store = pltpu.make_async_copy(sums, out.at[0], out_sems.at[0])
    store.start()
    store.wait()


def sandwich_sum(energy, pieces, blocks, shape):
    size = shape[-1]
    anywhere = pl.BlockSpec(memory_space=pl.ANY)
    return pl.pallas_call(
        kernel,
        out_shape=jax.ShapeDtypeStruct(shape, jnp.float32),
        in_specs=[pl.BlockSpec(memory_space=pltpu.SMEM)] + [anywhere] * 9,
        out_specs=anywhere,
        scratch_shapes=[
            pltpu.VMEM((2, 4, 2, size // 4, size), jnp.float32),
            pltpu.VMEM((4, 2, size, size), jnp.float32),
            pltpu.VMEM((2, 2, size, size), jnp.float32),
            pltpu.VMEM((2, 3, size, 3 * size), jnp.bfloat16),
            pltpu.SemaphoreType.DMA((5,)),
            pltpu.SemaphoreType.DMA((4,)),
            pltpu.SemaphoreType.DMA((2,)),
        ],
        cost_estimate=pl.CostEstimate(flops=144 * size**3, bytes_accessed=16 * size * size * 4, transcendentals=0),
        name="sandwich_sum",
    )(energy, *pieces, *blocks)


def shards(green_blocks, couplings, owners, momentum_shift, energy_shift):
    n_kz, n_en = sizes()
    local = green_blocks.shape[1]
    pieces = cut_couplings(*part_of_both_cores(couplings[0, 0]), owners)
    pieces, green_blocks = lax.optimization_barrier((pieces, green_blocks))
    value = scatter_couplings(pieces, owners)
    assert n_kz & (n_kz - 1) == 0 and n_en & (n_en - 1) == 0
    count = MAX_SHIFT
    energy, momentum = energy_shift, momentum_shift
    energy_other, momentum_other = energy[::-1], momentum[::-1]
    low, high = jnp.minimum(energy, energy_other), jnp.maximum(energy, energy_other)
    first = jnp.where(energy > energy_other, momentum_other, momentum)
    more = jnp.where(energy_other > energy, momentum_other - momentum, momentum - momentum_other)
    lead = jnp.arange(2) == 0
    steps = jnp.where(lead, first, more) & (n_kz - 1)
    rise = jnp.where(lead, low - 1, high - low)
    index = steps * count + rise
    blocks = tuple(green_blocks[:, i : i + 1] for i in range(local))
    en_rest = [("en", bit) for bit in range(1, (n_en - 1).bit_length())]
    rest = en_rest + [("kz", bit) for bit in range(2, (n_kz - 1).bit_length())]

    def early(held, ops):
        value, owner = ops
        for step, (axis, bit) in enumerate(rest):
            other = send_bit(value, axis, bit)
            value = keep_bit(value, other, owner, axis, bit)
            if step == 0:
                last, value = lax.optimization_barrier((held[-1], value))
                held = held[:-1] + (last,)
        return held, value

    def late(held, value):
        pieces = [value] + [None] * 3
        for j in (3, 2, 1):
            pieces[j] = flip(value, j // 2 * 2, j % 2)
        return held, tuple(pieces) + (flip(jnp.stack(pieces), 1, 0),)

    blocks, index_first, index_more = lax.optimization_barrier((blocks, index[0], index[1]))
    near, value = move(blocks, index_first, 1, early, (value, owners))
    far, pieces = move(near, index_more, 0, late, value)
    return sandwich_sum(energy_shift, pieces, near + far, green_blocks.shape)


def solution(mesh):
    in_specs = (P("kz", "en", None, None, None), P("kz", "en", None, None, None), P(), P(), P())
    out_specs = P("kz", "en", None, None, None)
    return jax.shard_map(shards, mesh=mesh, in_specs=in_specs, out_specs=out_specs, check_vma=False)
```
